32 devices in a mesh: section: 4 (over y, x), expert: 8 (over z, core).
Axes of the slice: x: 2, y: 2, z: 4, core: 2. Of those that a mesh axis runs over, the one named last changes fastest.
Arguments:
- saved_inputs: bfloat16 [4, 2, 96, 3072], P('section', None, 'expert'), may hold values from -6 to 6
- expert_ids: int32 [4, 2, 96, 2], P('section'), may hold values from 0 to 3, all different within a row; in each aligned block of 12 rows (0 to 11, 12 to 23, ..., all dimensions but the last counted through in order) at most 9 rows name the same one
- combine: bfloat16 [4, 2, 96, 2], P('section'), may hold values from 0.19921875 to 1
- top_grad: bfloat16 [2, 96, 3072], P(None, 'expert'), may hold values from -6 to 6
- w_gate: bfloat16 [4, 3072, 32768], P('section', None, 'expert'), may hold values from -0.109375 to 0.109375
- w_up: bfloat16 [4, 3072, 32768], P('section', None, 'expert'), may hold values from -0.109375 to 0.109375
- w_down: bfloat16 [4, 32768, 3072], P('section', 'expert'), may hold values from -0.0625 to 0.0625
Outputs:
- input_grads: bfloat16 [4, 2, 96, 3072], P('section', None, 'expert')
- combine_grads: float32 [4, 2, 96, 2], P('section', None, 'expert')
The draws below stay inside these ranges and needn't reach their ends.
Inputs may be any that keep to these rules, and one draw needn't show every extreme that they name: `expert_ids`: each token names 2 different experts. Among the 12 tokens of one index of expert in one layer and micro-batch, no expert is named more than 9 times, and some expert reaches 9.
All inputs are finite; a program needn't handle non-finite values.
Results may differ from the reference program's by a relative error of at most 0.018.
Values may be sent and summed in bfloat16 or wider, within the bound.
No kernel may reach another device: no remote copies, remote signals or barrier semaphores. Data moves between devices by JAX's collectives and lax.ppermute only.
A program may use at most 192 MiB of HBM per device.

```python
import math
import jax
import jax.numpy as jnp
import numpy as np
from jax import lax

D = 3072
FF = 8192
EXPERTS = 4
TOP = 2
MB = 2
TOK_MB = 12
CAP = 9
SECTIONS = 4
TOKENS = 96
FF_DEV = 4096
N_EXPERT = 8


def steps_of(own_key, shape, shards, low, largest):
    factor_of = 1.0
    for axis_at, parts in shards:
        draws = jax.random.uniform(jax.random.fold_in(jax.random.fold_in(own_key, 6), axis_at), (parts,), jnp.float32, low / len(shards), largest / len(shards))
        factor_of = factor_of * jnp.repeat(jnp.exp(draws), shape[axis_at] // parts).reshape((-1,) + (1,) * (len(shape) - 1 - axis_at))
    return factor_of


def routed_block(rng, own, number, rows, number_of, top, reach, skew):
    order = jax.random.permutation(rng, number_of)
    packed, ordinary = shares(number_of, rows * top, reach, skew, True), shares(number_of, rows * top, reach, skew, False)
    places = jnp.arange(number_of)

    def named(tallies, offset_by):
        used = int((tallies > 0).sum())
        fixed = max(1, used // 4)
        passed = fixed + (places - fixed + offset_by * (used - fixed)) % max(1, number_of - fixed)
        return jnp.zeros((number_of,), jnp.int32).at[order[jnp.where(places < fixed, places, passed)]].set(jnp.asarray(tallies, jnp.int32))

    tallies = jnp.where(number % 4 == 0, named(packed, number // 4), named(ordinary, number - number // 4 - 1))
    mixed = jax.random.permutation(jax.random.fold_in(own, 3), number_of)
    source_of, sink = mixed[0:number_of // 2 * 2:2], mixed[1:number_of // 2 * 2:2]
    slack = jnp.minimum(tallies[source_of] - 1, reach - tallies[sink]) // 2
    slack = jnp.where((source_of == order[0]) | (sink == order[0]) | (tallies[sink] == 0), 0, jnp.maximum(slack, 0))
    passed = jax.random.randint(jax.random.fold_in(own, 4), (number_of // 2,), 0, 1 << 20) % (slack + 1)
    tallies = tallies.at[source_of].add(-passed).at[sink].add(passed)
    items = jnp.searchsorted(jnp.cumsum(tallies), jnp.arange(rows * top), side="right").astype(jnp.int32)
    listing = items.reshape(top, rows).T
    listing = listing[jax.random.permutation(jax.random.fold_in(own, 1), rows)]
    offset_by = jax.random.randint(jax.random.fold_in(own, 2), (rows, 1), 0, top)
    return jnp.take_along_axis(listing, (jnp.arange(top)[None, :] + offset_by) % top, axis=1)


def shares(number_of, total, reach, lean, full):
    portions = [(1 << 20) // math.isqrt(rank ** lean) + 1 for rank in range(1, number_of + 1)]
    largest = reach if full else min(reach, max(-(-total // number_of), total * portions[0] // sum(portions)))
    least = 1 if total - largest >= number_of - 1 else 0
    given, rest = [largest] + [least] * (number_of - 1), total - largest - least * (number_of - 1)
    while rest > 0:
        candidates = [i for i in range(1, number_of) if given[i] < largest] or [i for i in range(1, number_of) if given[i] < reach]
        mass, budget = sum([portions[i] for i in candidates]), rest
        for i in candidates:
            addition = min(reach - given[i], max(1, budget * portions[i] // mass), rest)
            given[i] = given[i] + addition
            rest = rest - addition
    return np.array(given)


def centred(rng, shape, width, reach, split=(), kind=jnp.bfloat16):
    array = jax.random.normal(rng, shape, jnp.float32) * width
    if len(split) > 0:
        array = steps_of(rng, shape, split, -0.22, 0.18) * array
    return jnp.clip(array, min=-reach, max=reach).astype(kind)


def setup_inputs(seed: int = 0) -> dict:
    streams_of = jax.random.split(jax.random.key(seed), 8)
    saved_inputs = centred(streams_of[0], (SECTIONS, MB, TOKENS, D), 1.0, 6.0, ((0, 4), (2, 8)))
    expert_ids_keys = jax.random.split(jax.random.fold_in(streams_of[1], 1), SECTIONS * MB * TOKENS // TOK_MB)
    expert_ids_turns = jax.random.permutation(jax.random.fold_in(streams_of[1], 3), SECTIONS * MB * TOKENS // TOK_MB)
    expert_ids = jax.vmap(lambda own, number: routed_block(jax.random.fold_in(streams_of[1], 2), own, number, TOK_MB, EXPERTS, TOP, CAP, 2))(expert_ids_keys, expert_ids_turns).reshape((SECTIONS, MB, TOKENS, TOP))
    combine = jnp.clip(0.19921875 + 0.80078125 * jax.random.uniform(streams_of[2], (SECTIONS, MB, TOKENS, TOP), jnp.float32) ** steps_of(streams_of[2], (SECTIONS, MB, TOKENS, TOP), ((0, 4),), -0.2, 0.2), 0.19921875, 1.0).astype(jnp.bfloat16)
    top_grad = centred(streams_of[3], (MB, TOKENS, D), 1.0, 6.0, ((1, 8),))
    w_gate = centred(streams_of[4], (SECTIONS, D, EXPERTS * FF), D ** -0.5, 0.109375, ((0, 4), (2, 8)))
    w_up = centred(streams_of[5], (SECTIONS, D, EXPERTS * FF), D ** -0.5, 0.109375, ((0, 4), (2, 8)))
    w_down = centred(streams_of[6], (SECTIONS, EXPERTS * FF, D), FF ** -0.5, 0.0625, ((0, 4), (1, 8)))
    return dict(saved_inputs=saved_inputs, expert_ids=expert_ids, combine=combine, top_grad=top_grad, w_gate=w_gate, w_up=w_up, w_down=w_down)


def silu_parts(values):
    sig = jax.nn.sigmoid(values)
    return values * sig, sig * (1.0 + values * (1.0 - sig))


def round_half(values):
    return lax.optimization_barrier(values.astype(jnp.bfloat16)).astype(jnp.float32)


def expert_rows(inputs, grads, weights, gate_part, lift_part, down_part):
    pre_gate = jnp.dot(inputs, gate_part, preferred_element_type=jnp.float32)
    pre_lift = jnp.dot(inputs, lift_part, preferred_element_type=jnp.float32)
    hidden_grad = jnp.dot(grads, down_part.T, preferred_element_type=jnp.float32)
    active, slope = silu_parts(pre_gate)
    product = hidden_grad * active * pre_lift
    scaled = weights[:, None] * hidden_grad
    gate_grad = (scaled * pre_lift * slope).astype(jnp.bfloat16)
    lift_grad = (scaled * active).astype(jnp.bfloat16)
    moved = jnp.zeros((inputs.shape[0], inputs.shape[1]), jnp.float32)
    slot_grads = jnp.zeros((inputs.shape[0],), jnp.float32)
    for piece in range(FF // FF_DEV):
        lower = piece * FF_DEV
        upper_end = lower + FF_DEV
        part = jnp.dot(gate_grad[:, lower:upper_end], gate_part[:, lower:upper_end].T, preferred_element_type=jnp.float32)
        part = part + jnp.dot(lift_grad[:, lower:upper_end], lift_part[:, lower:upper_end].T, preferred_element_type=jnp.float32)
        moved = moved + round_half(part)
        slot_grads = slot_grads + round_half(jnp.sum(product[:, lower:upper_end], axis=-1))
    return moved, slot_grads


def reference(saved_inputs, expert_ids, combine, top_grad, w_gate, w_up, w_down):
    limit = N_EXPERT * CAP
    incoming = [top_grad[m] for m in range(MB)]
    layer_grads = [None] * SECTIONS
    layer_slots = [None] * SECTIONS
    for layer in reversed(range(SECTIONS)):
        outs_grad = []
        outs_slot = []
        for m in range(MB):
            inputs = saved_inputs[layer, m]
            upper = incoming[m]
            chosen = expert_ids[layer, m].reshape(-1)
            weights = combine[layer, m].reshape(-1).astype(jnp.float32)
            total = upper.astype(jnp.float32)
            slot_total = jnp.zeros((TOKENS * TOP,), jnp.float32)
            for expert in range(EXPERTS):
                match = chosen == expert
                picked = jnp.nonzero(match, size=limit, fill_value=0)[0].astype(jnp.int32)
                live = (jnp.arange(limit, dtype=jnp.int32) < jnp.sum(match.astype(jnp.int32))).astype(jnp.float32)
                rows = (picked // TOP).astype(jnp.int32)
                gate_part = w_gate[layer][:, expert * FF:(expert + 1) * FF]
                lift_part = w_up[layer][:, expert * FF:(expert + 1) * FF]
                down_part = w_down[layer][expert * FF:(expert + 1) * FF, :]
                moved, slot_grads = expert_rows(inputs[rows], upper[rows], weights[picked] * live, gate_part, lift_part, down_part)
                total = total.at[rows].add(moved * live[:, None])
                slot_total = slot_total.at[picked].add(slot_grads * live)
            outs_grad.append(total.astype(jnp.bfloat16))
            outs_slot.append(slot_total.reshape(TOKENS, TOP))
        layer_grads[layer] = jnp.stack(outs_grad)
        layer_slots[layer] = jnp.stack(outs_slot)
        incoming = outs_grad
    return jnp.stack(layer_grads), jnp.stack(layer_slots)
```

```python
import jax
import jax.numpy as jnp
from jax import lax
from jax.sharding import PartitionSpec as P

EXPERTS = 4


def silu_parts(values):
    sig = jax.nn.sigmoid(values)
    return (values * sig, sig * (1.0 + values * (1.0 - sig)))


def per_device(saved_inputs, expert_ids, combine, top_grad, w_gate, w_up, w_down):
    devices = lax.axis_size("expert")
    sections = lax.axis_size("section")
    lanes = devices // 2
    me = lax.axis_index("expert")
    my_section = lax.axis_index("section")
    my_lane, my_core = me // 2, me % 2
    own_expert = me // (devices // EXPERTS)
    gate_part, lift_part, down_part = w_gate[0], w_up[0], w_down[0]
    micro, tokens, width = saved_inputs.shape[1:]
    choose = expert_ids.shape[3]
    block = micro * tokens

    def to_core(rows):
        return lax.ppermute(rows, "expert", [(i, i ^ 1) for i in range(devices)])

    def to_lane(rows, k):
        return lax.ppermute(rows, "expert", [(i, i ^ (2 * k)) for i in range(devices)])

    def to_lower_lane(rows, k):
        pairs = [
            (s * devices + i, (s - 1) * devices + (i ^ (2 * k)))
            for s in range(1, sections)
            for i in range(devices)
        ]
        return lax.ppermute(rows, ("section", "expert"), pairs)

    def both_cores(mine):
        return jnp.concatenate([mine, to_core(mine)], axis=0)

    def gather(rows):
        return both_cores(
            jnp.concatenate([rows] + [to_lane(rows, k) for k in range(1, lanes)], axis=0)
        )

    lane_of = my_lane ^ jnp.arange(lanes)
    core_of = my_core ^ jnp.arange(2)
    source = (lane_of[None, :] * 2 + core_of[:, None]).reshape(-1)
    chosen = jnp.moveaxis(expert_ids[0].reshape(micro, devices, tokens, choose), 1, 0)
    weight = jnp.moveaxis(combine[0].reshape(micro, devices, tokens, choose), 1, 0)
    routed = jnp.sum(
        jnp.where(chosen == own_expert, weight.astype(jnp.float32), 0.0), axis=-1
    )
    routed = jnp.take(routed, source, axis=0).reshape(-1)

    inputs = gather(saved_inputs[0].reshape(block, width))
    upper = top_grad.reshape(block, width)
    upper_all = gather(upper)
    pre_gate = jnp.dot(inputs, gate_part, preferred_element_type=jnp.float32)
    pre_lift = jnp.dot(inputs, lift_part, preferred_element_type=jnp.float32)
    active, slope = silu_parts(pre_gate)
    to_gate = routed[:, None] * pre_lift * slope
    to_lift = routed[:, None] * active
    to_slot = active * pre_lift

    grads_out = jnp.zeros((block, width), jnp.bfloat16)
    slots_all = jnp.zeros((devices * block,), jnp.float32)
    for step in range(sections):
        valid = my_section == sections - 1 - step
        hidden = lax.dot_general(
            upper_all, down_part, (((1,), (1,)), ((), ())), preferred_element_type=jnp.float32
        )
        slots = jnp.sum(hidden * to_slot, axis=-1)
        slots_all = jnp.where(valid, slots, slots_all)
        gate_grad = (hidden * to_gate).astype(jnp.bfloat16)
        lift_grad = (hidden * to_lift).astype(jnp.bfloat16)
        moved = jnp.einsum("rf,df->rd", gate_grad, gate_part, preferred_element_type=jnp.float32)
        moved = moved + jnp.einsum(
            "rf,df->rd", lift_grad, lift_part, preferred_element_type=jnp.float32
        )
        half = lanes * block
        sent = moved[half:].astype(jnp.bfloat16)
        pair = (moved[:half] + to_core(sent).astype(jnp.float32)).reshape(lanes, block, width)
        total = upper.astype(jnp.float32) + pair[0]
        for k in range(1, lanes):
            total = total + to_lane(pair[k].astype(jnp.bfloat16), k).astype(jnp.float32)
        result = total.astype(jnp.bfloat16)
        grads_out = jnp.where(valid, result, grads_out)
        if step < sections - 1:
            arrived = [to_lower_lane(result, k) for k in range(lanes)]
            upper = arrived[0]
            upper_all = both_cores(jnp.concatenate(arrived, axis=0))

    half = lanes * block
    pair = slots_all[:half].astype(jnp.bfloat16).astype(jnp.float32) + to_core(
        slots_all[half:].astype(jnp.bfloat16)
    ).astype(jnp.float32)
    pair = pair.reshape(lanes, block)
    mine = [pair[0]] + [to_lane(pair[k], k) for k in range(1, lanes)]
    expert_of = (lane_of * 2) // (devices // EXPERTS)
    own_chosen = lax.dynamic_index_in_dim(chosen, me, 0, keepdims=False).reshape(block, choose)
    slots_out = jnp.zeros((block, choose), jnp.float32)
    for k in range(lanes):
        slots_out = slots_out + jnp.where(own_chosen == expert_of[k], mine[k][:, None], 0.0)
    return (
        grads_out.reshape(1, micro, tokens, width),
        slots_out.reshape(1, micro, tokens, choose),
    )


def solution(mesh):
    placed = (
        P("section", None, "expert", None),
        P("section", None, None, None),
        P("section", None, None, None),
        P(None, "expert", None),
        P("section", None, "expert"),
        P("section", None, "expert"),
        P("section", "expert", None),
    )
    return jax.shard_map(
        per_device,
        mesh=mesh,
        in_specs=placed,
        out_specs=(P("section", None, "expert", None), P("section", None, "expert", None)),
        check_vma=False,
    )
```

```python
import functools

import jax
import jax.numpy as jnp
from jax import lax
from jax.experimental import pallas as pl
from jax.experimental.pallas import tpu as pltpu
from jax.sharding import PartitionSpec as P


EXPERTS = 4
CHUNKS = 2
ROWS_DOT = (((1,), (1,)), ((), ()))
VMEM_SPEC = pl.BlockSpec(memory_space=pltpu.VMEM)
SMEM_SPEC = pl.BlockSpec(memory_space=pltpu.SMEM)
ANY_SPEC = pl.BlockSpec(memory_space=pl.ANY)


def silu_parts(values):
    sig = jax.nn.sigmoid(values)
    return (values * sig, sig * (1.0 + values * (1.0 - sig)))


def tile_of(total, wanted):
    while total % wanted:
        wanted //= 2
    return wanted


def hidden_kernel(pieces, column, tile, depth, first, last, active, *refs):
    @pl.when(active[0] == 1)
    def _():
        hidden_body(pieces, column, tile, depth, first, last, list(refs))


def hidden_body(pieces, column, tile, depth, first, last, refs):
    parts = [refs.pop(0) for _ in range(pieces)]
    weight = refs.pop(0)
    streamed = [] if first else [refs.pop(0)]
    if last:
        streamed += [refs.pop(0) for _ in range(3)]
        gate_grad, lift_grad, slots = refs.pop(0), refs.pop(0), refs.pop(0)
    else:
        hidden = refs.pop(0)
    grads, buffer, sems = refs.pop(0), refs.pop(0), refs.pop(0)
    side, side_sems = refs if streamed else (None, None)
    block, width = parts[0].shape
    steps = weight.shape[0] // tile

    def weight_copy(i, slot):
        rows = weight.at[pl.ds(i * tile, tile), pl.ds(column, width)]
        return pltpu.make_async_copy(rows, buffer.at[slot], sems.at[slot])

    def side_copies(i, slot):
        cols = pl.ds(pl.multiple_of(i * tile, tile), tile)
        return [
            pltpu.make_async_copy(ref.at[:, cols], side.at[slot, j], side_sems.at[slot, j])
            for j, ref in enumerate(streamed)
        ]

    for i in range(min(depth - 1, steps)):
        weight_copy(i, i).start()
    for copy in side_copies(0, 0):
        copy.start()
    for j, part in enumerate(parts):
        grads[j * block : (j + 1) * block, :] = part[...]
    if last:
        slots[...] = jnp.zeros_like(slots)

    @pl.loop(0, steps)
    def _(i):
        slot, side_slot = lax.rem(i, depth), lax.rem(i, 2)

        @pl.when(i + depth - 1 < steps)
        def _():
            weight_copy(i + depth - 1, lax.rem(i + depth - 1, depth)).start()

        @pl.when(i + 1 < steps)
        def _():
            for copy in side_copies(i + 1, 1 - side_slot):
                copy.start()

        weight_copy(i, slot).wait()
        got = lax.dot_general(
            grads[...], buffer[slot], ROWS_DOT, preferred_element_type=jnp.float32
        )
        for copy in side_copies(i, side_slot):
            copy.wait()
        if not first:
            got = got + side[side_slot, 0]
        cols = pl.ds(pl.multiple_of(i * tile, tile), tile)
        if last:
            at = len(streamed) - 3
            gate_grad[:, cols] = (got * side[side_slot, at]).astype(jnp.bfloat16)
            lift_grad[:, cols] = (got * side[side_slot, at + 1]).astype(jnp.bfloat16)
            slots[...] += jnp.sum(got * side[side_slot, at + 2], axis=1, keepdims=True)
        else:
            hidden[:, cols] = got


def hidden_part(active, parts, weight, column, before, factors):
    block, width = parts[0].shape
    rows, units = block * len(parts), weight.shape[0]
    tile, depth = tile_of(units, 512), 4
    last = factors is not None
    streamed = ([] if before is None else [before]) + (list(factors) if last else [])
    if last:
        outs = (jax.ShapeDtypeStruct((rows, units), jnp.bfloat16),) * 2 + (
            jax.ShapeDtypeStruct((rows, 1), jnp.float32),
        )
    else:
        outs = (jax.ShapeDtypeStruct((rows, units), jnp.float32),)
    scratch = [
        pltpu.VMEM((rows, width), jnp.bfloat16),
        pltpu.VMEM((depth, tile, width), jnp.bfloat16),
        pltpu.SemaphoreType.DMA((depth,)),
    ]
    if streamed:
        scratch += [
            pltpu.VMEM((2, len(streamed), rows, tile), jnp.float32),
            pltpu.SemaphoreType.DMA((2, len(streamed))),
        ]
    return pl.pallas_call(
        functools.partial(
            hidden_kernel, len(parts), column, tile, depth, before is None, last
        ),
        in_specs=[SMEM_SPEC] + [VMEM_SPEC] * len(parts) + [ANY_SPEC] * (1 + len(streamed)),
        out_specs=(VMEM_SPEC,) * len(outs),
        out_shape=outs,
        scratch_shapes=scratch,
        cost_estimate=pl.CostEstimate(
            flops=2 * rows * width * units,
            bytes_accessed=2 * width * units + 4 * rows * units * len(streamed),
            transcendentals=0,
        ),
        compiler_params=pltpu.CompilerParams(vmem_limit_bytes=36 * 2**20),
    )(active, *parts, weight, *streamed)


def moved_kernel(row, tile, depth, active, *refs):
    @pl.when(active[0] == 1)
    def _():
        moved_body(row, tile, depth, *refs)


def moved_body(row, tile, depth, gate_grad, lift_grad, gate, lift, keep, send, bufs, sems):
    steps = keep.shape[1] // tile
    half = keep.shape[0]

    def copies(i, slot):
        rows = pl.ds(row + i * tile, tile)
        return [
            pltpu.make_async_copy(ref.at[rows], bufs.at[slot, j], sems.at[slot, j])
            for j, ref in enumerate((gate, lift))
        ]

    for i in range(min(depth - 1, steps)):
        for copy in copies(i, i):
            copy.start()

    @pl.loop(0, steps)
    def _(i):
        slot = lax.rem(i, depth)

        @pl.when(i + depth - 1 < steps)
        def _():
            for copy in copies(i + depth - 1, lax.rem(i + depth - 1, depth)):
                copy.start()

        first, second = copies(i, slot)
        first.wait()
        got = lax.dot_general(
            gate_grad[...], bufs[slot, 0], ROWS_DOT, preferred_element_type=jnp.float32
        )
        second.wait()
        got = got + lax.dot_general(
            lift_grad[...], bufs[slot, 1], ROWS_DOT, preferred_element_type=jnp.float32
        )
        cols = pl.ds(pl.multiple_of(i * tile, tile), tile)
        keep[:, cols] = got[:half]
        send[:, cols] = got[half:].astype(jnp.bfloat16)


def moved_part(active, gate_grad, lift_grad, gate, lift, row, width):
    rows, units = gate_grad.shape
    tile, depth = tile_of(width, 256), 3
    half = rows // 2
    return pl.pallas_call(
        functools.partial(moved_kernel, row, tile, depth),
        in_specs=[SMEM_SPEC, VMEM_SPEC, VMEM_SPEC, ANY_SPEC, ANY_SPEC],
        out_specs=(VMEM_SPEC, VMEM_SPEC),
        out_shape=(
            jax.ShapeDtypeStruct((half, width), jnp.float32),
            jax.ShapeDtypeStruct((half, width), jnp.bfloat16),
        ),
        scratch_shapes=[
            pltpu.VMEM((depth, 2, tile, units), jnp.bfloat16),
            pltpu.SemaphoreType.DMA((depth, 2)),
        ],
        cost_estimate=pl.CostEstimate(
            flops=4 * rows * width * units, bytes_accessed=4 * width * units, transcendentals=0
        ),
        compiler_params=pltpu.CompilerParams(vmem_limit_bytes=28 * 2**20),
    )(active, gate_grad, lift_grad, gate, lift)


def per_device(saved_inputs, expert_ids, combine, top_grad, w_gate, w_up, w_down):
    devices = lax.axis_size("expert")
    sections = lax.axis_size("section")
    lanes = devices // 2
    me = lax.axis_index("expert")
    my_section = lax.axis_index("section")
    my_lane, my_core = me // 2, me % 2
    own_expert = me // (devices // EXPERTS)
    gate_part, lift_part, down_part = w_gate[0], w_up[0], w_down[0]
    micro, tokens, width = saved_inputs.shape[1:]
    choose = expert_ids.shape[3]
    block = micro * tokens
    half = lanes * block
    chunk = width // CHUNKS

    def to_core(rows):
        return lax.ppermute(rows, "expert", [(i, i ^ 1) for i in range(devices)])

    def to_lane(rows, k):
        return lax.ppermute(rows, "expert", [(i, i ^ (2 * k)) for i in range(devices)])

    def to_lower_lane(rows, k):
        pairs = [
            (s * devices + i, (s - 1) * devices + (i ^ (2 * k)))
            for s in range(1, sections)
            for i in range(devices)
        ]
        return lax.ppermute(rows, ("section", "expert"), pairs)

    def gather(rows):
        mine = [rows] + [to_lane(rows, k) for k in range(1, lanes)]
        return mine + [to_core(part) for part in mine]

    def own_slots(sums):
        other = to_core(sums[half:].astype(jnp.bfloat16)).astype(jnp.float32)
        pair = sums[:half].astype(jnp.bfloat16).astype(jnp.float32) + other
        pair = pair.reshape(lanes, block)
        mine = [pair[0]] + [to_lane(pair[k], k) for k in range(1, lanes)]
        expert_of = (lane_of * 2) // (devices // EXPERTS)
        own = lax.dynamic_index_in_dim(chosen, me, 0, keepdims=False).reshape(block, choose)
        out = jnp.zeros((block, choose), jnp.float32)
        for k in range(lanes):
            out = out + jnp.where(own == expert_of[k], mine[k][:, None], 0.0)
        return out

    lane_of = my_lane ^ jnp.arange(lanes)
    core_of = my_core ^ jnp.arange(2)
    source = (lane_of[None, :] * 2 + core_of[:, None]).reshape(-1)
    chosen = jnp.moveaxis(expert_ids[0].reshape(micro, devices, tokens, choose), 1, 0)
    weight = jnp.moveaxis(combine[0].reshape(micro, devices, tokens, choose), 1, 0)
    routed = jnp.sum(
        jnp.where(chosen == own_expert, weight.astype(jnp.float32), 0.0), axis=-1
    )
    routed = jnp.take(routed, source, axis=0).reshape(-1)

    mine = gather(saved_inputs[0].reshape(block, width))
    inputs = jnp.concatenate(mine, axis=0)
    pre_gate = jnp.dot(inputs, gate_part, preferred_element_type=jnp.float32)
    pre_lift = jnp.dot(inputs, lift_part, preferred_element_type=jnp.float32)
    active, slope = silu_parts(pre_gate)
    factors = (
        routed[:, None] * pre_lift * slope,
        routed[:, None] * active,
        active * pre_lift,
    )

    top, mine = lax.optimization_barrier((top_grad.reshape(block, width), mine))
    upper = [top[:, c * chunk : (c + 1) * chunk] for c in range(CHUNKS)]
    pieces = [gather(part) for part in upper]
    pieces, _ = lax.optimization_barrier((pieces, pre_gate))
    results = [jnp.zeros((block, chunk), jnp.bfloat16) for _ in range(CHUNKS)]
    slots_all = jnp.zeros((devices * block, 1), jnp.float32)
    turns = [my_section == sections - 1 - step for step in range(sections)]
    active = [turn.astype(jnp.int32).reshape(1) for turn in turns]
    hidden = hidden_part(active[0], pieces[0], down_part, 0, None, None)[0]
    for step in range(sections):
        valid = turns[step]
        gate_grad, lift_grad, slots = hidden_part(
            active[step], pieces[1], down_part, chunk, hidden, factors
        )
        slots_all = jnp.where(valid, slots, slots_all)
        if step == sections - 1:
            slots_out = own_slots(slots_all.reshape(-1))
        next_upper, pieces = [], []
        for c in range(CHUNKS):
            keep, send = moved_part(
                active[step],
                gate_grad,
                lift_grad,
                gate_part,
                lift_part,
                c * chunk,
                chunk,
            )
            pair = keep + to_core(send).astype(jnp.float32)
            pair = pair.reshape(lanes, block, chunk)
            back = [
                to_lane(pair[k].astype(jnp.bfloat16), k) for k in range(1, lanes)
            ]
            total = upper[c].astype(jnp.float32) + pair[0]
            for part in back:
                total = total + part.astype(jnp.float32)
            result = total.astype(jnp.bfloat16)
            results[c] = jnp.where(valid, result, results[c])
            if step < sections - 1:
                arrived = [to_lower_lane(result, k) for k in range(lanes)]
                pieces.append(arrived + [to_core(part) for part in arrived])
                next_upper.append(arrived[0])
        upper = next_upper
        if step < sections - 1:
            hidden = hidden_part(
                active[step + 1], pieces[0], down_part, 0, None, None
            )[0]

    return (
        jnp.concatenate(results, axis=1).reshape(1, micro, tokens, width),
        slots_out.reshape(1, micro, tokens, choose),
    )


def solution(mesh):
    placed = (
        P("section", None, "expert", None),
        P("section", None, None, None),
        P("section", None, None, None),
        P(None, "expert", None),
        P("section", None, "expert"),
        P("section", None, "expert"),
        P("section", "expert", None),
    )
    return jax.shard_map(
        per_device,
        mesh=mesh,
        in_specs=placed,
        out_specs=(P("section", None, "expert", None), P("section", None, "expert", None)),
        check_vma=False,
    )
```
